32 devices in a mesh: dp: 4 (over z), mp: 8 (over y, x, core).
Axes of the slice: x: 2, y: 2, z: 4, core: 2. Of those that a mesh axis runs over, the one named last changes fastest.
Arguments:
- activations: bfloat16 [1024, 12288], P('dp', 'mp'), may hold values from -6 to 6
- out_grad: bfloat16 [1024, 12288], P('dp', 'mp'), may hold values from -1.5 to 1.5
- up_blocks: bfloat16 [128, 4224, 128], P(None, 'mp'), may hold values from -0.15625 to 0.15625
- down_blocks: bfloat16 [128, 4224, 128], P(None, 'mp'), may hold values from -0.078125 to 0.078125
- latent_in: bfloat16 [256, 12288], P(None, 'mp'), may hold values from -0.0546875 to 0.0546875
- latent_out: bfloat16 [256, 49152], P(None, 'mp'), may hold values from -0.375 to 0.375
- block_rows: int32 [11, 384], P(None, 'mp'), may hold values from 0 to 95, as said below
- section_count: int32 [384], P('mp'), may hold values from 1 to 11, as said below
Outputs:
- mixed: bfloat16 [1024, 12288], P('dp', 'mp')
- input_grad: bfloat16 [1024, 12288], P('dp', 'mp')
- up_grad: bfloat16 [128, 4224, 128], P('dp', 'mp')
- down_grad: bfloat16 [128, 4224, 128], P('dp', 'mp')
- latent_in_grad: bfloat16 [256, 12288], P('dp', 'mp')
- latent_out_grad: bfloat16 [256, 49152], P('dp', 'mp')
The draws below stay inside these ranges and needn't reach their ends.
Inputs may be any that keep to these rules, and one draw needn't show every extreme that they name: `block_rows`: the 11 entries of one column are distinct feature blocks. `section_count`: on one index of mp every column has all 11 sections live.
All inputs are finite; a program needn't handle non-finite values.
Results may differ from the reference program's by a relative error of at most 0.02.
Values may be sent and summed in bfloat16 or wider, within the bound.
A program may use at most 320 MiB of HBM per device.

```python
import jax
import jax.numpy as jnp
from jax import lax

D = 12288
FF = 49152
BS = 128
RANK = 256
TOK_DEV = 256
TOKENS = 1024
DB = 96
FB = 384
NCAND = 11
COLS = 48
SLOTS = 528
NBLK = 4224
N_DP = 4
N_MP = 8


def draw_block_rows(key, part):
    home_rows = jax.random.randint(jax.random.fold_in(key, 11), (FB,), 0, DB)
    home_rows = jnp.where(jnp.arange(FB) == 0, 0, home_rows)
    section_at = jnp.arange(NCAND)
    level_at = jnp.maximum(section_at - 1, 0) // 2
    stride = jnp.left_shift(jnp.ones_like(level_at), level_at) * jnp.where(section_at % 2 == 1, 1, -1) * (section_at > 0)
    return ((home_rows[None, :] + stride[:, None]) % DB).astype(jnp.int32)


def draw_section_count(key, part):
    device_top = jax.random.randint(jax.random.fold_in(key, 21), (N_MP,), NCAND // 2 + 1, NCAND + 1)
    busiest = jax.random.randint(jax.random.fold_in(key, 22), (), 0, N_MP)
    device_top = jnp.where(jnp.arange(N_MP) == busiest, NCAND, device_top)
    drop_by = jax.random.randint(jax.random.fold_in(key, 23), (FB,), 0, 3)
    owner_of = jnp.arange(FB) // COLS
    counts = jnp.maximum(device_top[owner_of] - drop_by, 1)
    counts = jnp.where(owner_of == busiest, NCAND, counts)
    lowest = (busiest + 1) % N_MP * COLS
    counts = jnp.where(jnp.arange(FB) == lowest, 1, counts)
    return counts.astype(jnp.int32)


def steps_of(own_key, dims, split, least, largest):
    level = 1.0
    for position, shards_of in split:
        heights = jax.random.uniform(jax.random.fold_in(jax.random.fold_in(own_key, 6), position), (shards_of,), jnp.float32, least / len(split), largest / len(split))
        level = level * jnp.repeat(jnp.exp(heights), dims[position] // shards_of).reshape((-1,) + (1,) * (len(dims) - 1 - position))
    return level


def normal_values(own_key, shape, deviation, limit, cuts=(), dtype=jnp.bfloat16):
    values = deviation * jax.random.normal(own_key, shape, jnp.float32)
    if cuts:
        values = values * steps_of(own_key, shape, cuts, -0.22, 0.18)
    return jnp.clip(values, -limit, limit).astype(dtype)


def setup_inputs(seed: int = 0) -> dict:
    splits = jax.random.split(jax.random.key(seed), 9)
    activations = normal_values(splits[0], (TOKENS, D), 1.0, 6.0, ((0, 4), (1, 8)))
    out_grad = normal_values(splits[1], (TOKENS, D), 0.25, 1.5, ((0, 4), (1, 8)))
    up_blocks = normal_values(splits[2], (BS, NBLK, BS), (BS * NCAND) ** -0.5, 0.15625, ((1, 8),))
    down_blocks = normal_values(splits[3], (BS, NBLK, BS), (BS * NCAND * FB // DB) ** -0.5, 0.078125, ((1, 8),))
    latent_in = normal_values(splits[4], (RANK, D), D ** -0.5, 0.0546875, ((1, 8),))
    latent_out = normal_values(splits[5], (RANK, FF), RANK ** -0.5, 0.375, ((1, 8),))
    block_rows = draw_block_rows(jax.random.fold_in(splits[8], 71), 0)
    section_count = draw_section_count(jax.random.fold_in(splits[8], 71), 0)
    return dict(activations=activations, out_grad=out_grad, up_blocks=up_blocks, down_blocks=down_blocks, latent_in=latent_in, latent_out=latent_out, block_rows=block_rows, section_count=section_count)


gelu_coef = 0.044715
gelu_scale = 0.7978845608028654


def gelu_parts(preact):
    inside = gelu_scale * (preact + gelu_coef * preact * preact * preact)
    tanh_part = jnp.tanh(inside)
    activated = 0.5 * preact * (1.0 + tanh_part)
    derivative = 0.5 * (1.0 + tanh_part) + 0.5 * preact * (1.0 - tanh_part * tanh_part) * gelu_scale * (1.0 + 3.0 * gelu_coef * preact * preact)
    return activated, derivative


def rounded(source):
    return lax.optimization_barrier(source.astype(jnp.bfloat16)).astype(jnp.float32)


def grouped(source):
    return source.reshape((N_DP, TOK_DEV) + source.shape[1:])


def reference(activations, out_grad, up_blocks, down_blocks, latent_in, latent_out, block_rows, section_count):
    in_blocks = activations.reshape(TOKENS, DB, BS).astype(jnp.float32)
    grad_blocks = out_grad.reshape(TOKENS, DB, BS).astype(jnp.float32)
    latent = jnp.dot(activations, latent_in.T, preferred_element_type=jnp.float32).astype(jnp.bfloat16)
    latent_float = latent.astype(jnp.float32)
    up_owned = jnp.transpose(up_blocks.reshape(BS, N_MP, SLOTS, BS), (1, 0, 2, 3))
    down_owned = jnp.transpose(down_blocks.reshape(BS, N_MP, SLOTS, BS), (1, 0, 2, 3))
    rows_owned = jnp.transpose(block_rows.reshape(NCAND, N_MP, COLS), (1, 0, 2))
    count_owned = section_count.reshape(N_MP, COLS)
    latent_owned = jnp.transpose(latent_out.reshape(RANK, N_MP, COLS * BS), (1, 0, 2))

    def owner_pass(running, pieces):
        out_total, in_total, back_total = running
        up_own, down_own, rows_own, count_own, latent_own = pieces
        up_float = up_own.astype(jnp.float32)
        down_float = down_own.astype(jnp.float32)
        live_list = [(section_at < count_own).astype(jnp.float32)[None, :, None] for section_at in range(NCAND)]
        sparse_pre = jnp.zeros((TOKENS, COLS, BS), jnp.float32)
        for section_at in range(NCAND):
            picked = jnp.take(in_blocks, rows_own[section_at], axis=1)
            weights = up_float[:, section_at * COLS:(section_at + 1) * COLS, :]
            sparse_pre = sparse_pre + jnp.einsum("rck,kcn->rcn", picked, weights) * live_list[section_at]
        preact = sparse_pre.reshape(TOKENS, COLS * BS) + jnp.dot(latent, latent_own, preferred_element_type=jnp.float32)
        activated, derivative = gelu_parts(preact)
        hidden = activated.astype(jnp.bfloat16)
        hidden_float = hidden.astype(jnp.float32).reshape(TOKENS, COLS, BS)
        out_part = jnp.zeros((TOKENS, DB, BS), jnp.float32)
        hidden_grad = jnp.zeros((TOKENS, COLS, BS), jnp.float32)
        down_list = []
        for section_at in range(NCAND):
            weights = down_float[:, section_at * COLS:(section_at + 1) * COLS, :]
            live_now = live_list[section_at]
            picked_grad = jnp.take(grad_blocks, rows_own[section_at], axis=1)
            out_part = out_part.at[:, rows_own[section_at], :].add(jnp.einsum("rck,kcn->rcn", hidden_float, weights) * live_now)
            hidden_grad = hidden_grad + jnp.einsum("rcn,kcn->rck", picked_grad, weights) * live_now
            group_terms = jnp.einsum("grck,grcn->gkcn", grouped(hidden_float), grouped(picked_grad))
            down_list.append(jnp.sum(rounded(group_terms), axis=0) * live_now[0])
        pre_grad = (hidden_grad.reshape(TOKENS, COLS * BS) * derivative).astype(jnp.bfloat16)
        pre_float = pre_grad.astype(jnp.float32).reshape(TOKENS, COLS, BS)
        back_total = back_total + jnp.dot(pre_grad, latent_own.T, preferred_element_type=jnp.float32)
        in_part = jnp.zeros((TOKENS, DB, BS), jnp.float32)
        up_list = []
        for section_at in range(NCAND):
            weights = up_float[:, section_at * COLS:(section_at + 1) * COLS, :]
            live_now = live_list[section_at]
            picked = jnp.take(in_blocks, rows_own[section_at], axis=1)
            in_part = in_part.at[:, rows_own[section_at], :].add(jnp.einsum("rcn,kcn->rck", pre_float, weights) * live_now)
            group_terms = jnp.einsum("grck,grcn->gkcn", grouped(picked), grouped(pre_float))
            up_list.append(jnp.sum(rounded(group_terms), axis=0) * live_now[0])
        latent_terms = jnp.einsum("grk,grn->gkn", grouped(latent_float), grouped(pre_grad.astype(jnp.float32)))
        latent_grad = jnp.sum(rounded(latent_terms), axis=0).astype(jnp.bfloat16)
        out_total = out_total + rounded(out_part)
        in_total = in_total + rounded(in_part)
        up_grad = jnp.concatenate(up_list, axis=1).astype(jnp.bfloat16)
        down_grad = jnp.concatenate(down_list, axis=1).astype(jnp.bfloat16)
        return (out_total, in_total, back_total), (up_grad, down_grad, latent_grad)

    zero_feat = jnp.zeros((TOKENS, DB, BS), jnp.float32)
    start_state = (zero_feat, zero_feat, jnp.zeros((TOKENS, RANK), jnp.float32))
    final_state, stacks = lax.scan(owner_pass, start_state, (up_owned, down_owned, rows_owned, count_owned, latent_owned))
    out_total, in_total, back_total = final_state
    up_stack, down_stack, latent_stack = stacks
    mixed = out_total.reshape(TOKENS, D).astype(jnp.bfloat16)
    back_latent = back_total.astype(jnp.bfloat16)
    input_grad = (in_total.reshape(TOKENS, D) + jnp.dot(back_latent, latent_in, preferred_element_type=jnp.float32)).astype(jnp.bfloat16)
    up_grad = jnp.transpose(up_stack, (1, 0, 2, 3)).reshape(BS, NBLK, BS)
    down_grad = jnp.transpose(down_stack, (1, 0, 2, 3)).reshape(BS, NBLK, BS)
    latent_out_grad = jnp.transpose(latent_stack, (1, 0, 2)).reshape(RANK, FF)
    in_terms = jnp.einsum("grk,grd->gkd", grouped(back_latent.astype(jnp.float32)), grouped(activations.astype(jnp.float32)))
    latent_in_grad = jnp.sum(rounded(in_terms), axis=0).astype(jnp.bfloat16)
    return (mixed, input_grad, up_grad, down_grad, latent_in_grad, latent_out_grad)
```

```python
import functools

import jax
import jax.numpy as jnp
from jax import lax
from jax.experimental import pallas as pl
from jax.experimental.pallas import tpu as pltpu
from jax.sharding import PartitionSpec as P

gelu_coef = 0.044715
gelu_scale = 0.7978845608028654
vmem_limit = 60 * 1024 * 1024
bf16 = jnp.bfloat16
f32 = jnp.float32
last_last = (((1,), (1,)), ((), ()))
first_first = (((0,), (0,)), ((), ()))


def gelu_parts(preact):
    inside = gelu_scale * (preact + gelu_coef * preact * preact * preact)
    tanh_part = jnp.tanh(inside)
    activated = 0.5 * preact * (1.0 + tanh_part)
    derivative = 0.5 * (1.0 + tanh_part) + 0.5 * preact * (
        1.0 - tanh_part * tanh_part
    ) * gelu_scale * (1.0 + 3.0 * gelu_coef * preact * preact)
    return (activated, derivative)


def picked_blocks(rows_ref, source_ref, column, sections, axis):
    return jnp.concatenate(
        [source_ref[rows_ref[section_at, column]] for section_at in range(sections)], axis=axis
    )


def forward_kernel(
    sections, rows_ref, in_ref, grad_ref, up_ref, down_ref, latent_ref, lout_ref, hid_ref, pre_ref
):
    column = pl.program_id(0)
    in_wide = picked_blocks(rows_ref, in_ref, column, sections, 1)
    preact = jnp.dot(in_wide, up_ref[0], preferred_element_type=f32) + jnp.dot(
        latent_ref[...], lout_ref[...], preferred_element_type=f32
    )
    activated, derivative = gelu_parts(preact)
    hid_ref[...] = activated.astype(bf16)
    grad_wide = picked_blocks(rows_ref, grad_ref, column, sections, 1)
    hidden_grad = lax.dot_general(grad_wide, down_ref[0], last_last, preferred_element_type=f32)
    pre_ref[...] = (hidden_grad * derivative).astype(bf16)


def spread_kernel(
    sections,
    width,
    rows_ref,
    grad_ref,
    up_ref,
    down_ref,
    hid_ref,
    pre_ref,
    lout_ref,
    mask_ref,
    mixed_ref,
    back_ref,
    dgrad_ref,
    lat_ref,
    out_total,
    in_total,
    lat_total,
):
    column = pl.program_id(0)
    row_blocks = out_total.shape[0]

    @pl.when(column == 0)
    def _():
        @pl.loop(0, row_blocks)
        def _(block_at):
            out_total[block_at] = jnp.zeros(out_total.shape[1:], f32)
            in_total[block_at] = jnp.zeros(in_total.shape[1:], f32)

        lat_total[...] = jnp.zeros_like(lat_total)

    hidden = hid_ref[...]
    pre = pre_ref[...]
    grad_wide = picked_blocks(rows_ref, grad_ref, column, sections, 1)
    weight_grad = lax.dot_general(hidden, grad_wide, first_first, preferred_element_type=f32)
    weight_grad = (weight_grad * mask_ref[0]).astype(bf16)
    dgrad_ref[...] = weight_grad.reshape(dgrad_ref.shape)
    forward = jnp.dot(hidden, down_ref[0], preferred_element_type=f32)
    backward = lax.dot_general(pre, up_ref[0], last_last, preferred_element_type=f32)
    for section_at in range(sections):
        row = rows_ref[section_at, column]
        cut = slice(section_at * width, (section_at + 1) * width)
        out_total[row] += forward[:, cut]
        in_total[row] += backward[:, cut]
    lat_total[...] += lax.dot_general(pre, lout_ref[...], last_last, preferred_element_type=f32)

    @pl.when(column == pl.num_programs(0) - 1)
    def _():
        @pl.loop(0, row_blocks)
        def _(block_at):
            mixed_ref[block_at] = out_total[block_at].astype(bf16)
            back_ref[block_at] = in_total[block_at].astype(bf16)

        lat_ref[...] = lat_total[...].astype(bf16)


def up_grad_kernel(
    sections, rows_ref, count_ref, part_ref, latent_ref, pre_ref, ugrad_ref, lgrad_ref
):
    column = pl.program_id(0)
    pre = pre_ref[...].reshape(-1, pre_ref.shape[-1])
    part_rows = part_ref.shape[1]
    stacked = picked_blocks(rows_ref, part_ref, column, sections, 0)
    product = jnp.dot(stacked, pre, preferred_element_type=f32)
    for section_at in range(sections):
        live = (section_at < count_ref[column]).astype(f32)
        ugrad_ref[0, section_at] = (
            product[section_at * part_rows : (section_at + 1) * part_rows] * live
        ).astype(bf16)
    lgrad_ref[...] = jnp.dot(latent_ref[...], pre, preferred_element_type=f32).astype(bf16)


def whole_spec():
    return pl.BlockSpec(memory_space=pltpu.VMEM)


def latent_total(partial_value):
    parts = lax.all_gather(partial_value.astype(bf16), "mp", axis=0)
    return jnp.sum(parts.astype(f32), axis=0).astype(bf16)


def shards(
    activations, out_grad, up_blocks, down_blocks, latent_in, latent_out, block_rows, section_count
):
    n_dp = lax.axis_size("dp")
    tok_rows, feat_local = activations.shape
    width = up_blocks.shape[0]
    columns = section_count.shape[0]
    sections = block_rows.shape[0]
    own_blocks = feat_local // width
    rank = latent_in.shape[0]
    hidden_width = columns * width
    span = sections * width
    cut_rows = width // n_dp
    rank_rows = rank // n_dp

    def by_block(values):
        return jnp.transpose(values.reshape(tok_rows, own_blocks, width), (1, 0, 2))

    def from_blocks(values):
        return jnp.transpose(values, (1, 0, 2)).reshape(tok_rows, feat_local)

    in_blocks = lax.all_gather(by_block(activations), "mp", axis=0, tiled=True)
    latent = latent_total(
        lax.dot_general(activations, latent_in, last_last, preferred_element_type=f32)
    )
    grad_blocks = lax.all_gather(by_block(out_grad), "mp", axis=0, tiled=True)
    sliced = jnp.transpose(
        activations.reshape(tok_rows, own_blocks, n_dp, cut_rows), (2, 1, 3, 0)
    )
    exchanged = lax.all_to_all(sliced, "dp", split_axis=0, concat_axis=0, tiled=True)
    exchanged = jnp.transpose(exchanged, (1, 2, 0, 3)).reshape(
        own_blocks, cut_rows, n_dp * tok_rows
    )
    exchanged, grad_blocks = lax.optimization_barrier((exchanged, grad_blocks))
    in_cuts = lax.all_gather(exchanged, "mp", axis=0, tiled=True)
    row_blocks = in_blocks.shape[0]

    live = jnp.arange(sections)[:, None] < section_count[None, :]
    live_slots = live.reshape(1, sections * columns, 1)
    zero = jnp.zeros((), bf16)
    up_live = jnp.where(live_slots, up_blocks, zero).reshape(width, sections, columns, width)
    down_live = jnp.where(live_slots, down_blocks, zero).reshape(width, sections, columns, width)
    up_cols = jnp.transpose(up_live, (2, 1, 0, 3)).reshape(columns, span, width)
    down_cols = jnp.transpose(down_live, (2, 0, 1, 3)).reshape(columns, width, span)
    mask = jnp.repeat(live.T.astype(f32), width, axis=1).reshape(columns, 1, span)

    def column_block(height):
        return pl.BlockSpec((height, width), lambda column, *_: (0, column))

    up_spec = pl.BlockSpec((1, span, width), lambda column, *_: (column, 0, 0))
    down_spec = pl.BlockSpec((1, width, span), lambda column, *_: (column, 0, 0))
    params = pltpu.CompilerParams(
        dimension_semantics=("arbitrary",), vmem_limit_bytes=vmem_limit
    )
    slab = jax.ShapeDtypeStruct((tok_rows, hidden_width), bf16)
    pair_flops = 2 * tok_rows * hidden_width * span
    weight_bytes = 2 * width * width * sections * columns

    hidden, pre_grad = pl.pallas_call(
        functools.partial(forward_kernel, sections),
        grid_spec=pltpu.PrefetchScalarGridSpec(
            num_scalar_prefetch=1,
            grid=(columns,),
            in_specs=[
                whole_spec(),
                whole_spec(),
                up_spec,
                down_spec,
                whole_spec(),
                column_block(rank),
            ],
            out_specs=[column_block(tok_rows), column_block(tok_rows)],
        ),
        out_shape=[slab, slab],
        compiler_params=params,
        cost_estimate=pl.CostEstimate(
            flops=2 * pair_flops, bytes_accessed=3 * weight_bytes, transcendentals=0
        ),
        name="forward",
    )(block_rows, in_blocks, grad_blocks, up_cols, down_cols, latent, latent_out)

    in_cuts, pre_sent = lax.optimization_barrier((in_cuts, pre_grad))
    pre_all = lax.all_gather(pre_sent, "dp", axis=0)

    totals = jax.ShapeDtypeStruct((row_blocks, tok_rows, width), bf16)
    mixed_part, in_part, down_part, back_part = pl.pallas_call(
        functools.partial(spread_kernel, sections, width),
        grid_spec=pltpu.PrefetchScalarGridSpec(
            num_scalar_prefetch=1,
            grid=(columns,),
            in_specs=[
                whole_spec(),
                up_spec,
                down_spec,
                column_block(tok_rows),
                column_block(tok_rows),
                column_block(rank),
                pl.BlockSpec((1, 1, span), lambda column, *_: (column, 0, 0)),
            ],
            out_specs=[
                whole_spec(),
                whole_spec(),
                pl.BlockSpec((n_dp, 1, cut_rows, span), lambda column, *_: (0, column, 0, 0)),
                whole_spec(),
            ],
            scratch_shapes=[
                pltpu.VMEM((row_blocks, tok_rows, width), f32),
                pltpu.VMEM((row_blocks, tok_rows, width), f32),
                pltpu.VMEM((tok_rows, rank), f32),
            ],
        ),
        out_shape=[
            totals,
            totals,
            jax.ShapeDtypeStruct((n_dp, columns, cut_rows, span), bf16),
            jax.ShapeDtypeStruct((tok_rows, rank), bf16),
        ],
        compiler_params=params,
        cost_estimate=pl.CostEstimate(
            flops=3 * pair_flops, bytes_accessed=4 * weight_bytes, transcendentals=0
        ),
        name="spread",
    )(block_rows, grad_blocks, up_cols, down_cols, hidden, pre_grad, latent_out, mask)

    pre_all, mixed_part, in_part, down_part, back_part = lax.optimization_barrier(
        (pre_all, mixed_part, in_part, down_part, back_part)
    )
    back_latent = latent_total(back_part)
    down_share = lax.psum_scatter(down_part, "dp", scatter_dimension=0, tiled=True)
    down_share, mixed_part, in_part = lax.optimization_barrier((down_share, mixed_part, in_part))
    mixed = from_blocks(lax.psum_scatter(mixed_part, "mp", scatter_dimension=0, tiled=True))
    input_sum = from_blocks(
        lax.psum_scatter(in_part, "mp", scatter_dimension=0, tiled=True).astype(f32)
    )
    input_grad = (
        input_sum + jnp.dot(back_latent, latent_in, preferred_element_type=f32)
    ).astype(bf16)
    down_share = jnp.transpose(
        down_share.reshape(columns, cut_rows, sections, width), (1, 2, 0, 3)
    ).reshape(cut_rows, sections * columns, width)

    latent_all = lax.all_gather(latent, "dp", axis=0)
    latent_cut = lax.dynamic_slice_in_dim(
        latent_all, lax.axis_index("dp") * rank_rows, rank_rows, 2
    )
    latent_cut = jnp.transpose(latent_cut, (2, 0, 1)).reshape(rank_rows, n_dp * tok_rows)

    up_part, lout_share = pl.pallas_call(
        functools.partial(up_grad_kernel, sections),
        grid_spec=pltpu.PrefetchScalarGridSpec(
            num_scalar_prefetch=2,
            grid=(columns,),
            in_specs=[
                whole_spec(),
                whole_spec(),
                pl.BlockSpec((n_dp, tok_rows, width), lambda column, *_: (0, 0, column)),
            ],
            out_specs=[
                pl.BlockSpec((1, sections, cut_rows, width), lambda column, *_: (column, 0, 0, 0)),
                column_block(rank_rows),
            ],
        ),
        out_shape=[
            jax.ShapeDtypeStruct((columns, sections, cut_rows, width), bf16),
            jax.ShapeDtypeStruct((rank_rows, hidden_width), bf16),
        ],
        compiler_params=params,
        cost_estimate=pl.CostEstimate(
            flops=pair_flops, bytes_accessed=weight_bytes, transcendentals=0
        ),
        name="up_grad",
    )(block_rows, section_count, in_cuts, latent_cut, pre_all)
    up_share = jnp.transpose(up_part, (2, 1, 0, 3)).reshape(cut_rows, sections * columns, width)

    latent_in_part = lax.dot_general(
        back_latent, activations, first_first, preferred_element_type=f32
    )
    lin_share = lax.psum_scatter(
        latent_in_part.astype(bf16), "dp", scatter_dimension=0, tiled=True
    )
    return (mixed, input_grad, up_share, down_share, lin_share, lout_share)


def solution(mesh):
    return jax.shard_map(
        shards,
        mesh=mesh,
        in_specs=(
            P("dp", "mp"),
            P("dp", "mp"),
            P(None, "mp", None),
            P(None, "mp", None),
            P(None, "mp"),
            P(None, "mp"),
            P(None, "mp"),
            P("mp"),
        ),
        out_specs=(
            P("dp", "mp"),
            P("dp", "mp"),
            P("dp", "mp", None),
            P("dp", "mp", None),
            P("dp", "mp"),
            P("dp", "mp"),
        ),
        check_vma=False,
    )
```
